32 devices in a mesh: wide: 8 (over z, y), narrow: 4 (over x, core).
Axes of the slice: x: 2, y: 2, z: 4, core: 2. Of those that a mesh axis runs over, the one named last changes fastest.
Arguments:
- op_blocks: bfloat16 [512, 6, 192, 192], P('wide', None, 'narrow'), may hold values from -6 to 6
- prolong: bfloat16 [512, 9216], P('wide', 'narrow'), may hold values from -0.4375 to 0.4375
- col_index: int32 [512, 6], P('wide'), may hold values from 0 to 511, as said below
- slot_index: int32 [512, 6], P('wide'), may hold values from 0 to 7
- dest_owner: int32 [512, 1], P('wide'), may hold values from 0 to 7; in each aligned block of 64 rows (0 to 63, 64 to 127, ...) at most 16 rows name the same one
- dest_local: int32 [512], P('wide'), may hold values from 0 to 15
Outputs:
- coarse: float32 [128, 48, 384], P('wide', 'narrow')
The draws below stay inside these ranges and needn't reach their ends.
Inputs may be any that keep to these rules, and one draw needn't show every extreme that they name: `col_index`: the first column of each row is the row itself; every column lies in the block rows of the same wide index or of the one just before or after it. `dest_owner`: among the 64 rows of one wide index no owner is named more than 16 times; some owner is named exactly 16 times.
All inputs are finite; a program needn't handle non-finite values.
Results may differ from the reference program's by a relative error of at most 0.0029.
Values may be sent and summed in bfloat16 or wider, within the bound.
A program may use at most 128 MiB of HBM per device.

```python
import math
import jax
import jax.numpy as jnp
import numpy as np
from jax import lax

B = 192
M = 48
K = 6
KC = 8
RB_DEV = 64
AGG_DEV = 16
CAP = 16
NFINE = 512
N_WIDE = 8


def draw_col_index(key, part):
    rows = jnp.arange(NFINE, dtype=jnp.int32)
    start = rows // RB_DEV * RB_DEV
    offsets = jax.random.randint(key, (NFINE, K), -RB_DEV, 2 * RB_DEV, dtype=jnp.int32)
    columns = start[:, None] + offsets
    columns = jnp.where(columns < 0, columns + RB_DEV, columns)
    columns = jnp.where(columns >= NFINE, columns - RB_DEV, columns)
    first = jnp.arange(K, dtype=jnp.int32)[None, :] == 0
    return jnp.where(first, rows[:, None], columns).astype(jnp.int32)


def with_ends(values, key, smallest, high):
    index_at = [jax.random.randint(jax.random.fold_in(key, axis), (), 0, length) for axis, length in enumerate(values.shape)]
    main_axis = values.shape.index(max(values.shape))
    neighbour = index_at[:main_axis] + [(index_at[main_axis] + 1) % values.shape[main_axis]] + index_at[main_axis + 1:]
    return values.at[tuple(index_at)].set(smallest).at[tuple(neighbour)].set(high)


def block_levels(key, dims, cuts, least, largest):
    def one(axis_at, blocks):
        heights = jax.random.uniform(jax.random.fold_in(jax.random.fold_in(key, 6), axis_at), (blocks,), jnp.float32, least / len(cuts), largest / len(cuts))
        return jnp.repeat(jnp.exp(heights), dims[axis_at] // blocks).reshape((-1,) + (1,) * (len(dims) - axis_at - 1))

    level = one(*cuts[0])
    for cut in cuts[1:]:
        level = level * one(*cut)
    return level


def shared_out(stream_key, own, number, rows, count, top, bound, slope):
    ranking = jax.random.permutation(stream_key, count)
    packed, common = shares(count, rows * top, bound, slope, True), shares(count, rows * top, bound, slope, False)
    places = jnp.arange(count)

    def named(tallies, turn):
        used = int((tallies > 0).sum())
        fixed = max(1, used // 4)
        shifted = fixed + (places - fixed + turn * (used - fixed)) % max(1, count - fixed)
        return jnp.zeros((count,), jnp.int32).at[ranking[jnp.where(places < fixed, places, shifted)]].set(jnp.asarray(tallies, jnp.int32))

    tallies = jnp.where(number % 4 == 0, named(packed, number // 4), named(common, number - number // 4 - 1))
    mixed = jax.random.permutation(jax.random.fold_in(own, 3), count)
    donor, sink = mixed[0:count // 2 * 2:2], mixed[1:count // 2 * 2:2]
    slack = jnp.minimum(tallies[donor] - 1, bound - tallies[sink]) // 2
    slack = jnp.where((donor == ranking[0]) | (sink == ranking[0]) | (tallies[sink] == 0), 0, jnp.maximum(slack, 0))
    shifted = jax.random.randint(jax.random.fold_in(own, 4), (count // 2,), 0, 1 << 20) % (slack + 1)
    tallies = tallies.at[donor].add(-shifted).at[sink].add(shifted)
    items = jnp.searchsorted(jnp.cumsum(tallies), jnp.arange(rows * top), side="right").astype(jnp.int32)
    grid = items.reshape(top, rows).T
    grid = grid[jax.random.permutation(jax.random.fold_in(own, 1), rows)]
    turn = jax.random.randint(jax.random.fold_in(own, 2), (rows, 1), 0, top)
    return jnp.take_along_axis(grid, (jnp.arange(top)[None, :] + turn) % top, axis=1)


def shares(number_of, total, most, skew, full):
    portions = [(1 << 20) // math.isqrt(grade ** skew) + 1 for grade in range(1, number_of + 1)]
    largest = most if full else min(most, max(-(-total // number_of), total * portions[0] // sum(portions)))
    least = 1 if total - largest >= number_of - 1 else 0
    counts, rest = [largest] + [least] * (number_of - 1), total - largest - least * (number_of - 1)
    while rest > 0:
        candidates = [i for i in range(1, number_of) if counts[i] < largest] or [i for i in range(1, number_of) if counts[i] < most]
        mass, left = sum([portions[i] for i in candidates]), rest
        for i in candidates:
            extra = min(most - counts[i], max(1, left * portions[i] // mass), rest)
            counts[i] = counts[i] + extra
            rest = rest - extra
    return np.array(counts)


def gaussian(stream_key, dims, width, bound, shards=(), kind=jnp.bfloat16):
    factor_of = block_levels(stream_key, dims, shards, -0.22, 0.18) if shards else 1.0
    entries = jax.random.normal(stream_key, dims, jnp.float32) * width * factor_of
    return jnp.minimum(jnp.maximum(entries, -bound), bound).astype(kind)


def setup_inputs(seed: int = 0) -> dict:
    arg_keys = jax.random.split(jax.random.key(seed), 7)
    op_blocks = gaussian(arg_keys[0], (NFINE, K, B, B), 1.0, 6.0, ((0, 8), (2, 4)))
    prolong = gaussian(arg_keys[1], (NFINE, B * M), B ** -0.5, 0.4375, ((0, 8), (1, 4)))
    col_index = draw_col_index(jax.random.fold_in(arg_keys[6], 71), 0)
    slot_index = with_ends(jax.random.randint(arg_keys[3], (NFINE, K), 0, KC), jax.random.fold_in(arg_keys[3], 1), 0, KC - 1).astype(jnp.int32)
    dest_owner_keys = jax.random.split(jax.random.fold_in(arg_keys[4], 1), NFINE // RB_DEV)
    dest_owner_turns = jax.random.permutation(jax.random.fold_in(arg_keys[4], 3), NFINE // RB_DEV)
    dest_owner = jax.vmap(lambda own, number: shared_out(jax.random.fold_in(arg_keys[4], 2), own, number, RB_DEV, N_WIDE, 1, CAP, 2))(dest_owner_keys, dest_owner_turns).reshape((NFINE, 1))
    dest_local = with_ends(jax.random.randint(arg_keys[5], (NFINE,), 0, AGG_DEV), jax.random.fold_in(arg_keys[5], 1), 0, AGG_DEV - 1).astype(jnp.int32)
    return {"op_blocks": op_blocks, "prolong": prolong, "col_index": col_index, "slot_index": slot_index, "dest_owner": dest_owner, "dest_local": dest_local}


def reference(op_blocks, prolong, col_index, slot_index, dest_owner, dest_local):
    fine_count = op_blocks.shape[0]
    prolong_blocks = prolong.reshape(fine_count, B, M)
    agg = (dest_owner[:, 0] * AGG_DEV + dest_local).astype(jnp.int32)

    def galerkin_row(pieces):
        op_row, columns, slot_row, own_block = pieces
        gathered = jnp.take(prolong_blocks, columns, axis=0)
        applied = jnp.einsum('krb,kbm->krm', op_row.astype(jnp.float32), gathered.astype(jnp.float32),
                             precision=lax.Precision.HIGHEST).astype(jnp.bfloat16)
        projected = jnp.einsum('rc,krm->kcm', own_block.astype(jnp.float32), applied.astype(jnp.float32),
                               precision=lax.Precision.HIGHEST)
        selector = (slot_row[:, None] == jnp.arange(KC, dtype=jnp.int32)[None, :]).astype(jnp.float32)
        summed = jnp.einsum('ks,kcm->csm', selector, projected, precision=lax.Precision.HIGHEST)
        return summed.reshape(M, KC * M)

    rows_all = lax.map(galerkin_row, (op_blocks, col_index, slot_index, prolong_blocks))
    return jax.ops.segment_sum(rows_all, agg, num_segments=AGG_DEV * N_WIDE)
```

```python
import functools

import jax
import jax.numpy as jnp
from jax import lax
from jax.experimental import pallas as pl
from jax.experimental.pallas import tpu as pltpu
from jax.sharding import PartitionSpec as P

B = 192
M = 48
KC = 8
AGG_DEV = 16
LANES = 128
GROUP = 4
SEATS = 8
CUTS = 3
EIGHT = 8
MESH = pl.DeviceIdType.MESH
F32 = jnp.float32
BF16 = jnp.bfloat16
I32 = jnp.int32
NT = (((1,), (1,)), ((), ()))
TWIN, OWN, SKEW = 0, 1, 2
VIA_X = 3


def kernel(
    count, parts,
    col_ref, slot_ref, owner_ref, local_ref, raw_ref, op_hbm, out_ref,
    op_ref, rawf, flat, held, tall, spread, tmp, part, rx1, tx2, rx2, sm, rxs, meta, seats, expand, pk, rxw,
    op_sem, gs, gr, ns, nr, ys, yr, ws, wr, ks,
):
    wide = lax.axis_index("wide")
    me = lax.axis_index("narrow")
    near = me + 1 - 2 * (me % 2)
    far = (me + 2) % parts
    cross = (near + 2) % parts
    odd = wide % 2
    twin = wide + 1 - 2 * odd
    half = count // 2
    rows, terms, depth, _ = op_ref.shape
    side = M // parts
    cut = side // CUTS
    block = cut * AGG_DEV
    chunks = rows // EIGHT
    groups = rows // GROUP
    halves = groups // SEATS
    ahead = wide + 2 - 4 * odd
    has_ahead = (ahead >= 0) & (ahead < count)
    behind = wide - 2 + 4 * odd
    has_behind = (behind >= 0) & (behind < count)

    def remote(src, dst, s, r, target):
        return pltpu.make_async_remote_copy(
            src_ref=src, dst_ref=dst, send_sem=s, recv_sem=r, device_id=target, device_id_type=MESH
        )

    fetch = pltpu.make_async_copy(op_hbm, op_ref, op_sem)
    fetch.start()

    barrier = pltpu.get_barrier_semaphore()

    def hello(where):
        pl.semaphore_signal(barrier, inc=1, device_id=where, device_id_type=MESH)

    hello((wide, near))
    hello((wide, far))
    hello((twin, me))

    @pl.loop(1, half)
    def _(d):
        hello(((wide + 2 * d) % count, me))

    width = depth * M
    rawf[:, :width] = raw_ref[...].astype(F32)
    rawf[:, width:] = jnp.zeros((rows, LANES), F32)
    for b in range(depth):
        flat[pl.ds(b, rows, stride=depth), :] = rawf[:, b * M : b * M + LANES]
    eye = (
        lax.broadcasted_iota(I32, (M, M), 0) == lax.broadcasted_iota(I32, (M, M), 1)
    ).astype(F32).astype(BF16)
    step = EIGHT * depth
    for c in range(chunks):
        blocks = flat[c * step : (c + 1) * step, :M].astype(BF16)
        held[OWN, me, c] = lax.dot_general(eye, blocks, NT, preferred_element_type=F32).astype(BF16)
    meta[0] = jnp.zeros((8, LANES), F32)
    meta[0, :terms, :rows] = slot_ref[...].astype(F32)
    meta[0, terms : terms + 1, :rows] = owner_ref[...].astype(F32)
    meta[0, terms + 1 : terms + 2, :rows] = local_ref[...].astype(F32)

    pl.semaphore_wait(barrier, half + 2)

    def move(slot, kind, c, target, source, share):
        return remote(
            held.at[source, share, c], held.at[slot, share, c],
            gs.at[slot, kind, c], gr.at[slot, kind, c], target,
        )

    def along(slot, c):
        if slot == TWIN:
            return move(TWIN, 0, c, (twin, me), OWN, me)
        return move(SKEW, 0, c, (ahead, me), TWIN, me)

    def along_far(slot, c):
        if slot == TWIN:
            return move(TWIN, 1, c, (twin, me), OWN, far)
        return move(SKEW, 1, c, (ahead, me), TWIN, far)

    def to_far(slot, c):
        return move(slot, 1, c, (wide, far), slot, me)

    def to_near(slot, c):
        return move(slot, 2, c, (wide, near), slot, me)

    def far_to_near(slot, c):
        return move(slot, 3, c, (wide, near), slot, far)

    def by_x(c):
        return c >= chunks - VIA_X

    def keys():
        return remote(meta.at[0], meta.at[1], ks.at[0], ks.at[1], (twin, me))

    for c in range(chunks):
        along(TWIN, c).start()
        to_far(OWN, c).start()
        to_near(OWN, c).start()
    keys().start()

    c_at = lax.broadcasted_iota(I32, (M, 2 * LANES), 0)
    lane = lax.broadcasted_iota(I32, (M, 2 * LANES), 1)
    c_part = c_at // side
    c_in = c_at - c_part * side
    c_cut = c_in // cut
    c_seat = (c_part % 2) * CUTS + c_cut
    c_lane = (c_part // 2) * LANES + c_in - c_cut * cut
    for seat in range(SEATS):
        first_lane = c_lane + ((c_seat + seat) % SEATS) * (GROUP * cut)
        for j in range(GROUP):
            chosen = (lane == first_lane + j * cut).astype(F32).astype(BF16)
            for h in range(halves):
                i = (h * SEATS + seat) * GROUP + j
                spread[h * SEATS + seat, j * depth : (j + 1) * depth] = jnp.dot(
                    flat[i * depth : (i + 1) * depth, :M].astype(BF16), chosen,
                    preferred_element_type=F32,
                ).astype(BF16)

    base_of = {OWN: rows, TWIN: (1 - odd) * (2 * rows), SKEW: odd * (2 * rows)}

    def assemble(slot, c):
        base = base_of[slot] + c * EIGHT
        for i in range(EIGHT):
            tall[base + i] = jnp.concatenate(
                [held[slot, p, c, :, i * depth : (i + 1) * depth] for p in range(parts)], axis=1
            )

    def pair(slot, c):
        to_near(slot, c).wait()
        far_to_near(slot, c).wait()

    for t in range(chunks + 3):
        if t < chunks:
            to_far(OWN, t).wait_recv()
            far_to_near(OWN, t).start()
            if not by_x(t):
                along_far(TWIN, t).start()
            along(TWIN, t).wait_recv()
            to_near(TWIN, t).start()
            pl.when(has_ahead)(lambda: along(SKEW, t).start())
            if by_x(t):
                to_far(TWIN, t).start()
        c = t - 1
        if 0 <= c < chunks:
            pair(OWN, c)
            assemble(OWN, c)

            @pl.when(has_behind)
            def _():
                along(SKEW, c).wait_recv()
                to_near(SKEW, c).start()
                if by_x(c):
                    to_far(SKEW, c).start()
        c = t - 2
        if 0 <= c < chunks:
            (to_far if by_x(c) else along_far)(TWIN, c).wait_recv()
            far_to_near(TWIN, c).start()
            if not by_x(c):
                pl.when(has_ahead)(lambda: along_far(SKEW, c).start())
        c = t - 3
        if 0 <= c < chunks:
            pair(TWIN, c)
            assemble(TWIN, c)

            @pl.when(has_behind)
            def _():
                (to_far if by_x(c) else along_far)(SKEW, c).wait_recv()
                far_to_near(SKEW, c).start()

    keys().wait()
    at = lax.broadcasted_iota(I32, (1, LANES), 1)
    row_at = lax.broadcasted_iota(I32, (LANES, LANES), 0)
    for q in range(CUTS):
        for h in range(halves):
            seat = (at // (GROUP * cut) - ((me % 2) * CUTS + q) + SEATS) % SEATS
            row = (h * SEATS + seat) * GROUP + (at // cut) % GROUP
            picks = (row_at == row).astype(F32).astype(BF16)
            for who in range(2):
                seen = jnp.dot(meta[who].astype(BF16), picks, preferred_element_type=F32)
                key = (
                    seen[terms : terms + 1] * block
                    + (at % cut).astype(F32) * AGG_DEV
                    + seen[terms + 1 : terms + 2]
                )
                seats[who, q, h] = jnp.concatenate([seen[:terms], key, key], axis=0)

    @pl.when(has_behind)
    def _():
        for c in range(chunks):
            pair(SKEW, c)
            assemble(SKEW, c)

    fetch.wait()

    def first(q, h):
        return remote(part.at[cross, q, h], rx1.at[1, q, h], ns.at[0, q, h], nr.at[0, q, h], (wide, near))

    def second(q, h):
        return remote(part.at[near, q, h], rx1.at[0, q, h], ns.at[1, q, h], nr.at[1, q, h], (wide, near))

    def third(q, h):
        return remote(tx2.at[q, h], rx2.at[q, h], ns.at[2, q, h], nr.at[2, q, h], (wide, far))

    def fourth(q, h):
        return remote(sm.at[q, h], rxs.at[q, h], ys.at[q, h], yr.at[q, h], (twin, me))

    def relay(q, h):
        first(q, h).wait()
        tx2[q, h] = (part[far, q, h] + rx1[1, q, h]).astype(BF16)
        third(q, h).start()

    def finish(q, h):
        second(q, h).wait()
        third(q, h).wait()
        sm[q, h] = (part[me, q, h] + rx1[0, q, h] + rx2[q, h].astype(F32)).astype(BF16)
        fourth(q, h).start()

    tile = GROUP * depth
    tile_lane = lax.broadcasted_iota(I32, (M, tile), 1)
    shift = rows - wide * rows

    def products(h, seat):
        start = (h * SEATS + seat) * GROUP
        applied = []
        for k in range(terms):
            left = jnp.concatenate(
                [tall[jnp.maximum(col_ref[k, start + j] + shift, 0)] for j in range(GROUP)], axis=0
            )
            right = jnp.concatenate([op_ref[start + j, k] for j in range(GROUP)], axis=0)
            both = lax.dot_general(left, right, NT, preferred_element_type=F32)
            kept = both[(GROUP - 1) * M :]
            for j in range(GROUP - 2, -1, -1):
                kept = jnp.where(tile_lane < (j + 1) * depth, both[j * M : (j + 1) * M], kept)
            applied.append(kept.astype(BF16))
        tmp[seat] = jnp.dot(
            jnp.concatenate(applied, axis=0), spread[h * SEATS + seat], preferred_element_type=F32
        )

    seat_lane = lax.broadcasted_iota(I32, (M, LANES), 1) // (GROUP * cut)

    def deal(h):
        @pl.loop(0, terms)
        def _(k):
            r = pl.ds(pl.multiple_of(k * M, M), M)
            for pair_at in range(parts // 2):
                held_at = [tmp[s, r, pair_at * LANES : (pair_at + 1) * LANES] for s in range(SEATS)]
                bit = 1
                while bit < SEATS:
                    taken = (seat_lane // bit) % 2 == 1
                    held_at = [
                        jnp.where(taken, held_at[(s + bit) % SEATS], held_at[s]) for s in range(SEATS)
                    ]
                    bit *= 2
                for s in range(2 * CUTS):
                    part[pair_at * 2 + s // CUTS, s % CUTS, h, r] = held_at[-s % SEATS]

    for h in range(halves):
        for seat in range(SEATS):
            products(h, seat)
            if h > 0 and seat == SEATS // 2:
                relay(0, h - 1)
        deal(h)
        for q in range(CUTS):
            first(q, h).start()
            second(q, h).start()

    order = [(q, h) for q in range(CUTS) for h in range(halves)]
    for q, h in order[1:]:
        relay(q, h)

    def widen(who, source, q):
        @pl.loop(0, halves)
        def _(h):
            blocks = [source[q, h, k * M : (k + 1) * M].astype(F32) for k in range(terms)]
            slots = [seats[who, q, h, k : k + 1] for k in range(terms)]
            for s in range(KC):
                total = jnp.zeros((M, LANES), F32)
                for k in range(terms):
                    total = total + jnp.where(slots[k] == s, blocks[k], 0.0)
                expand[who, h, s * M : (s + 1) * M] = total.astype(BF16)

    place = lax.broadcasted_iota(I32, (block, LANES), 0)

    def dense(owner, q):
        total = jnp.zeros((block, KC * M), F32)
        for who in range(2):
            for h in range(halves):
                hot = seats[who, q, h, terms : terms + 1] == (place + owner * block).astype(F32)
                total = total + lax.dot_general(
                    hot.astype(F32).astype(BF16), expand[who, h], NT, preferred_element_type=F32
                )
        return total

    def send(q, d):
        return remote(pk.at[q, d], rxw.at[q, d], ws.at[q, d], wr.at[q, d], ((wide + 2 * d) % count, me))

    def turn(i):
        return 1 + (i + half // 2 - 1) % (half - 1)

    for h in range(halves):
        finish(0, h)
    for q in range(CUTS):
        if q + 1 < CUTS:
            for h in range(halves):
                finish(q + 1, h)
        widen(0, sm, q)
        for h in range(halves):
            fourth(q, h).wait()
        widen(1, rxs, q)

        @pl.loop(0, half - 1)
        def _(i):
            d = turn(i)
            pk[q, d] = dense((wide + 2 * d) % count, q).astype(BF16)
            send(q, d).start()

        out_ref[q * block : (q + 1) * block] = dense(wide, q)

    for q in range(CUTS):
        @pl.loop(0, half - 1)
        def _(i):
            d = turn(i)
            send(q, d).wait()
            out_ref[q * block : (q + 1) * block] += rxw[q, d].astype(F32)

    for c in range(chunks):
        along(TWIN, c).wait_send()
        to_far(OWN, c).wait_send()
        if by_x(c):
            to_far(TWIN, c).wait_send()
        else:
            along_far(TWIN, c).wait_send()

        @pl.when(has_ahead)
        def _():
            along(SKEW, c).wait_send()
            if not by_x(c):
                along_far(SKEW, c).wait_send()

        if by_x(c):
            pl.when(has_behind)(lambda: to_far(SKEW, c).wait_send())


def on_device(op_blocks, prolong, col_index, slot_index, dest_owner, dest_local):
    rows, terms, depth, _ = op_blocks.shape
    count = lax.axis_size("wide")
    parts = lax.axis_size("narrow")
    side = M // parts
    chunks = rows // EIGHT
    groups = rows // GROUP
    halves = groups // SEATS
    half = count // 2
    block = side // CUTS * AGG_DEV
    deep = terms * M
    vmem = pl.BlockSpec(memory_space=pltpu.VMEM)
    smem = pl.BlockSpec(memory_space=pltpu.SMEM)
    hbm = pl.BlockSpec(memory_space=pl.ANY)
    dma = pltpu.SemaphoreType.DMA
    unit = (CUTS, halves, deep, LANES)
    coarse = pl.pallas_call(
        functools.partial(kernel, count, parts),
        out_shape=jax.ShapeDtypeStruct((side * AGG_DEV, KC * M), F32),
        in_specs=[smem, vmem, vmem, vmem, vmem, hbm],
        out_specs=vmem,
        scratch_shapes=[
            pltpu.VMEM(op_blocks.shape, BF16),
            pltpu.VMEM((rows, depth * M + LANES), F32),
            pltpu.VMEM((rows * depth, LANES), F32),
            pltpu.VMEM((3, parts, chunks, M, EIGHT * depth), BF16),
            pltpu.VMEM((3 * rows, M, B), BF16),
            pltpu.VMEM((groups, GROUP * depth, 2 * LANES), BF16),
            pltpu.VMEM((SEATS, deep, 2 * LANES), F32),
            pltpu.VMEM((parts,) + unit, F32),
            pltpu.VMEM((2,) + unit, F32),
            pltpu.VMEM(unit, BF16),
            pltpu.VMEM(unit, BF16),
            pltpu.VMEM(unit, BF16),
            pltpu.VMEM(unit, BF16),
            pltpu.VMEM((2, 8, LANES), F32),
            pltpu.VMEM((2, CUTS, halves, 8, LANES), F32),
            pltpu.VMEM((2, halves, KC * M, LANES), BF16),
            pltpu.VMEM((CUTS, half, block, KC * M), BF16),
            pltpu.VMEM((CUTS, half, block, KC * M), BF16),
            dma,
            dma((3, 4, chunks)), dma((3, 4, chunks)),
            dma((3, CUTS, halves)), dma((3, CUTS, halves)),
            dma((CUTS, halves)), dma((CUTS, halves)),
            dma((CUTS, half)), dma((CUTS, half)), dma((2,)),
        ],
        compiler_params=pltpu.CompilerParams(
            collective_id=0, has_side_effects=True, vmem_limit_bytes=56 << 20
        ),
    )(
        col_index.T, slot_index.T, dest_owner.T, dest_local.reshape(1, -1), prolong, op_blocks
    )
    return coarse.reshape(side, AGG_DEV, KC * M).swapaxes(0, 1)


def solution(mesh):
    in_specs = (
        P("wide", None, "narrow", None),
        P("wide", "narrow"),
        P("wide", None),
        P("wide", None),
        P("wide", None),
        P("wide"),
    )
    out_specs = P("wide", "narrow", None)
    return jax.shard_map(
        on_device, mesh=mesh, in_specs=in_specs, out_specs=out_specs, check_vma=False
    )
```

```python
import functools

import jax
import jax.numpy as jnp
from jax import lax
from jax.experimental import pallas as pl
from jax.experimental.pallas import tpu as pltpu
from jax.sharding import PartitionSpec as P

B = 192
M = 48
KC = 8
AGG_DEV = 16
LANES = 128
GROUP = 4
SEATS = 8
CUTS = 3
EIGHT = 8
MESH = pl.DeviceIdType.MESH
F32 = jnp.float32
BF16 = jnp.bfloat16
I32 = jnp.int32
NT = (((1,), (1,)), ((), ()))
TWIN, OWN, SKEW = 0, 1, 2
VIA_X = 3


def kernel(
    count, parts,
    col_ref, slot_ref, owner_ref, local_ref, raw_ref, op_hbm, out_ref,
    op_ref, rawf, flat, held, tall, spread, tmp, part, rx1, tx2, rx2, sm, rxs, meta, seats, expand, pk, rxw,
    op_sem, gs, gr, ns, nr, ys, yr, ws, wr, ks,
):
    wide = lax.axis_index("wide")
    me = lax.axis_index("narrow")
    near = me + 1 - 2 * (me % 2)
    far = (me + 2) % parts
    cross = (near + 2) % parts
    odd = wide % 2
    twin = wide + 1 - 2 * odd
    half = count // 2
    rows, terms, depth, _ = op_ref.shape
    side = M // parts
    cut = side // CUTS
    block = cut * AGG_DEV
    chunks = rows // EIGHT
    groups = rows // GROUP
    halves = groups // SEATS
    ahead = wide + 2 - 4 * odd
    has_ahead = (ahead >= 0) & (ahead < count)
    behind = wide - 2 + 4 * odd
    has_behind = (behind >= 0) & (behind < count)

    def remote(src, dst, s, r, target):
        return pltpu.make_async_remote_copy(
            src_ref=src, dst_ref=dst, send_sem=s, recv_sem=r, device_id=target, device_id_type=MESH
        )

    fetch = pltpu.make_async_copy(op_hbm, op_ref, op_sem)
    fetch.start()

    barrier = pltpu.get_barrier_semaphore()

    def hello(where):
        pl.semaphore_signal(barrier, inc=1, device_id=where, device_id_type=MESH)

    hello((wide, near))
    hello((wide, far))
    hello((twin, me))

    @pl.loop(1, half)
    def _(d):
        hello(((wide + 2 * d) % count, me))

    width = depth * M
    rawf[:, :width] = raw_ref[...].astype(F32)
    rawf[:, width:] = jnp.zeros((rows, LANES), F32)
    for b in range(depth):
        flat[pl.ds(b, rows, stride=depth), :] = rawf[:, b * M : b * M + LANES]
    eye = (
        lax.broadcasted_iota(I32, (M, M), 0) == lax.broadcasted_iota(I32, (M, M), 1)
    ).astype(F32).astype(BF16)
    step = EIGHT * depth
    for c in range(chunks):
        blocks = flat[c * step : (c + 1) * step, :M].astype(BF16)
        held[OWN, me, c] = lax.dot_general(eye, blocks, NT, preferred_element_type=F32).astype(BF16)
    meta[0] = jnp.zeros((8, LANES), F32)
    meta[0, :terms, :rows] = slot_ref[...].astype(F32)
    meta[0, terms : terms + 1, :rows] = owner_ref[...].astype(F32)
    meta[0, terms + 1 : terms + 2, :rows] = local_ref[...].astype(F32)

    pl.semaphore_wait(barrier, half + 2)

    def move(slot, kind, c, target, source, share):
        return remote(
            held.at[source, share, c], held.at[slot, share, c],
            gs.at[slot, kind, c], gr.at[slot, kind, c], target,
        )

    def along(slot, c):
        if slot == TWIN:
            return move(TWIN, 0, c, (twin, me), OWN, me)
        return move(SKEW, 0, c, (ahead, me), TWIN, me)

    def along_far(slot, c):
        if slot == TWIN:
            return move(TWIN, 1, c, (twin, me), OWN, far)
        return move(SKEW, 1, c, (ahead, me), TWIN, far)

    def to_far(slot, c):
        return move(slot, 1, c, (wide, far), slot, me)

    def to_near(slot, c):
        return move(slot, 2, c, (wide, near), slot, me)

    def far_to_near(slot, c):
        return move(slot, 3, c, (wide, near), slot, far)

    def by_x(c):
        return c >= chunks - VIA_X

    def keys():
        return remote(meta.at[0], meta.at[1], ks.at[0], ks.at[1], (twin, me))

    for c in range(chunks):
        along(TWIN, c).start()
        to_far(OWN, c).start()
        to_near(OWN, c).start()
    keys().start()

    c_at = lax.broadcasted_iota(I32, (M, 2 * LANES), 0)
    lane = lax.broadcasted_iota(I32, (M, 2 * LANES), 1)
    c_part = c_at // side
    c_in = c_at - c_part * side
    c_cut = c_in // cut
    c_seat = (c_part % 2) * CUTS + c_cut
    c_lane = (c_part // 2) * LANES + c_in - c_cut * cut
    for seat in range(SEATS):
        first_lane = c_lane + ((c_seat + seat) % SEATS) * (GROUP * cut)
        for j in range(GROUP):
            chosen = (lane == first_lane + j * cut).astype(F32).astype(BF16)
            for h in range(halves):
                i = (h * SEATS + seat) * GROUP + j
                spread[h * SEATS + seat, j * depth : (j + 1) * depth] = jnp.dot(
                    flat[i * depth : (i + 1) * depth, :M].astype(BF16), chosen,
                    preferred_element_type=F32,
                ).astype(BF16)

    base_of = {OWN: rows, TWIN: (1 - odd) * (2 * rows), SKEW: odd * (2 * rows)}

    def assemble(slot, c):
        base = base_of[slot] + c * EIGHT
        for i in range(EIGHT):
            tall[base + i] = jnp.concatenate(
                [held[slot, p, c, :, i * depth : (i + 1) * depth] for p in range(parts)], axis=1
            )

    def pair(slot, c):
        to_near(slot, c).wait()
        far_to_near(slot, c).wait()

    for c in range(chunks):
        to_far(OWN, c).wait_recv()
        far_to_near(OWN, c).start()
        if not by_x(c):
            along_far(TWIN, c).start()
        along(TWIN, c).wait_recv()
        pl.when(has_ahead)(lambda: along(SKEW, c).start())
        if by_x(c):
            to_far(TWIN, c).start()
        to_near(TWIN, c).start()
    for c in range(chunks):
        @pl.when(has_behind)
        def _():
            along(SKEW, c).wait_recv()
            if by_x(c):
                to_far(SKEW, c).start()
            to_near(SKEW, c).start()

        (to_far if by_x(c) else along_far)(TWIN, c).wait_recv()
        if not by_x(c):
            pl.when(has_ahead)(lambda: along_far(SKEW, c).start())
        far_to_near(TWIN, c).start()
        pair(OWN, c)
        assemble(OWN, c)
    for c in range(chunks):
        pair(TWIN, c)
        assemble(TWIN, c)

        @pl.when(has_behind)
        def _():
            (to_far if by_x(c) else along_far)(SKEW, c).wait_recv()
            far_to_near(SKEW, c).start()

    keys().wait()
    at = lax.broadcasted_iota(I32, (1, LANES), 1)
    row_at = lax.broadcasted_iota(I32, (LANES, LANES), 0)
    for q in range(CUTS):
        for h in range(halves):
            seat = (at // (GROUP * cut) - ((me % 2) * CUTS + q) + SEATS) % SEATS
            row = (h * SEATS + seat) * GROUP + (at // cut) % GROUP
            picks = (row_at == row).astype(F32).astype(BF16)
            for who in range(2):
                seen = jnp.dot(meta[who].astype(BF16), picks, preferred_element_type=F32)
                key = (
                    seen[terms : terms + 1] * block
                    + (at % cut).astype(F32) * AGG_DEV
                    + seen[terms + 1 : terms + 2]
                )
                seats[who, q, h] = jnp.concatenate([seen[:terms], key, key], axis=0)

    @pl.when(has_behind)
    def _():
        for c in range(chunks):
            pair(SKEW, c)
            assemble(SKEW, c)

    fetch.wait()

    def first(q, h):
        return remote(part.at[cross, q, h], rx1.at[1, q, h], ns.at[0, q, h], nr.at[0, q, h], (wide, near))

    def second(q, h):
        return remote(part.at[near, q, h], rx1.at[0, q, h], ns.at[1, q, h], nr.at[1, q, h], (wide, near))

    def third(q, h):
        return remote(tx2.at[q, h], rx2.at[q, h], ns.at[2, q, h], nr.at[2, q, h], (wide, far))

    def fourth(q, h):
        return remote(sm.at[q, h], rxs.at[q, h], ys.at[q, h], yr.at[q, h], (twin, me))

    def relay(q, h):
        first(q, h).wait()
        tx2[q, h] = (part[far, q, h] + rx1[1, q, h]).astype(BF16)
        third(q, h).start()

    def finish(q, h):
        second(q, h).wait()
        third(q, h).wait()
        sm[q, h] = (part[me, q, h] + rx1[0, q, h] + rx2[q, h].astype(F32)).astype(BF16)
        fourth(q, h).start()

    tile = GROUP * depth
    tile_lane = lax.broadcasted_iota(I32, (M, tile), 1)
    shift = rows - wide * rows

    def products(h, seat):
        start = (h * SEATS + seat) * GROUP
        applied = []
        for k in range(terms):
            left = jnp.concatenate(
                [tall[jnp.maximum(col_ref[k, start + j] + shift, 0)] for j in range(GROUP)], axis=0
            )
            right = jnp.concatenate([op_ref[start + j, k] for j in range(GROUP)], axis=0)
            both = lax.dot_general(left, right, NT, preferred_element_type=F32)
            kept = both[(GROUP - 1) * M :]
            for j in range(GROUP - 2, -1, -1):
                kept = jnp.where(tile_lane < (j + 1) * depth, both[j * M : (j + 1) * M], kept)
            applied.append(kept.astype(BF16))
        tmp[seat] = jnp.dot(
            jnp.concatenate(applied, axis=0), spread[h * SEATS + seat], preferred_element_type=F32
        )

    seat_lane = lax.broadcasted_iota(I32, (M, LANES), 1) // (GROUP * cut)

    def deal(h):
        @pl.loop(0, terms)
        def _(k):
            r = pl.ds(pl.multiple_of(k * M, M), M)
            for pair_at in range(parts // 2):
                held_at = [tmp[s, r, pair_at * LANES : (pair_at + 1) * LANES] for s in range(SEATS)]
                bit = 1
                while bit < SEATS:
                    taken = (seat_lane // bit) % 2 == 1
                    held_at = [
                        jnp.where(taken, held_at[(s + bit) % SEATS], held_at[s]) for s in range(SEATS)
                    ]
                    bit *= 2
                for s in range(2 * CUTS):
                    part[pair_at * 2 + s // CUTS, s % CUTS, h, r] = held_at[-s % SEATS]

    for h in range(halves):
        for seat in range(SEATS):
            products(h, seat)
            if h > 0 and seat == SEATS // 2:
                relay(0, h - 1)
        deal(h)
        for q in range(CUTS):
            first(q, h).start()
            second(q, h).start()

    order = [(q, h) for q in range(CUTS) for h in range(halves)]
    for q, h in order[1:]:
        relay(q, h)

    def widen(who, source, q):
        @pl.loop(0, halves)
        def _(h):
            blocks = [source[q, h, k * M : (k + 1) * M].astype(F32) for k in range(terms)]
            slots = [seats[who, q, h, k : k + 1] for k in range(terms)]
            for s in range(KC):
                total = jnp.zeros((M, LANES), F32)
                for k in range(terms):
                    total = total + jnp.where(slots[k] == s, blocks[k], 0.0)
                expand[who, h, s * M : (s + 1) * M] = total.astype(BF16)

    place = lax.broadcasted_iota(I32, (block, LANES), 0)

    def dense(owner, q):
        total = jnp.zeros((block, KC * M), F32)
        for who in range(2):
            for h in range(halves):
                hot = seats[who, q, h, terms : terms + 1] == (place + owner * block).astype(F32)
                total = total + lax.dot_general(
                    hot.astype(F32).astype(BF16), expand[who, h], NT, preferred_element_type=F32
                )
        return total

    def send(q, d):
        return remote(pk.at[q, d], rxw.at[q, d], ws.at[q, d], wr.at[q, d], ((wide + 2 * d) % count, me))

    def turn(i):
        return 1 + (i + half // 2 - 1) % (half - 1)

    for h in range(halves):
        finish(0, h)
    for q in range(CUTS):
        if q + 1 < CUTS:
            for h in range(halves):
                finish(q + 1, h)
        widen(0, sm, q)
        for h in range(halves):
            fourth(q, h).wait()
        widen(1, rxs, q)

        @pl.loop(0, half - 1)
        def _(i):
            d = turn(i)
            pk[q, d] = dense((wide + 2 * d) % count, q).astype(BF16)
            send(q, d).start()

        out_ref[q * block : (q + 1) * block] = dense(wide, q)

    for q in range(CUTS):
        @pl.loop(0, half - 1)
        def _(i):
            d = turn(i)
            send(q, d).wait()
            out_ref[q * block : (q + 1) * block] += rxw[q, d].astype(F32)

    for c in range(chunks):
        along(TWIN, c).wait_send()
        to_far(OWN, c).wait_send()
        if by_x(c):
            to_far(TWIN, c).wait_send()
        else:
            along_far(TWIN, c).wait_send()

        @pl.when(has_ahead)
        def _():
            along(SKEW, c).wait_send()
            if not by_x(c):
                along_far(SKEW, c).wait_send()

        if by_x(c):
            pl.when(has_behind)(lambda: to_far(SKEW, c).wait_send())


def on_device(op_blocks, prolong, col_index, slot_index, dest_owner, dest_local):
    rows, terms, depth, _ = op_blocks.shape
    count = lax.axis_size("wide")
    parts = lax.axis_size("narrow")
    side = M // parts
    chunks = rows // EIGHT
    groups = rows // GROUP
    halves = groups // SEATS
    half = count // 2
    block = side // CUTS * AGG_DEV
    deep = terms * M
    vmem = pl.BlockSpec(memory_space=pltpu.VMEM)
    smem = pl.BlockSpec(memory_space=pltpu.SMEM)
    hbm = pl.BlockSpec(memory_space=pl.ANY)
    dma = pltpu.SemaphoreType.DMA
    unit = (CUTS, halves, deep, LANES)
    coarse = pl.pallas_call(
        functools.partial(kernel, count, parts),
        out_shape=jax.ShapeDtypeStruct((side * AGG_DEV, KC * M), F32),
        in_specs=[smem, vmem, vmem, vmem, vmem, hbm],
        out_specs=vmem,
        scratch_shapes=[
            pltpu.VMEM(op_blocks.shape, BF16),
            pltpu.VMEM((rows, depth * M + LANES), F32),
            pltpu.VMEM((rows * depth, LANES), F32),
            pltpu.VMEM((3, parts, chunks, M, EIGHT * depth), BF16),
            pltpu.VMEM((3 * rows, M, B), BF16),
            pltpu.VMEM((groups, GROUP * depth, 2 * LANES), BF16),
            pltpu.VMEM((SEATS, deep, 2 * LANES), F32),
            pltpu.VMEM((parts,) + unit, F32),
            pltpu.VMEM((2,) + unit, F32),
            pltpu.VMEM(unit, BF16),
            pltpu.VMEM(unit, BF16),
            pltpu.VMEM(unit, BF16),
            pltpu.VMEM(unit, BF16),
            pltpu.VMEM((2, 8, LANES), F32),
            pltpu.VMEM((2, CUTS, halves, 8, LANES), F32),
            pltpu.VMEM((2, halves, KC * M, LANES), BF16),
            pltpu.VMEM((CUTS, half, block, KC * M), BF16),
            pltpu.VMEM((CUTS, half, block, KC * M), BF16),
            dma,
            dma((3, 4, chunks)), dma((3, 4, chunks)),
            dma((3, CUTS, halves)), dma((3, CUTS, halves)),
            dma((CUTS, halves)), dma((CUTS, halves)),
            dma((CUTS, half)), dma((CUTS, half)), dma((2,)),
        ],
        compiler_params=pltpu.CompilerParams(
            collective_id=0, has_side_effects=True, vmem_limit_bytes=52 << 20
        ),
    )(
        col_index.T, slot_index.T, dest_owner.T, dest_local.reshape(1, -1), prolong, op_blocks
    )
    return coarse.reshape(side, AGG_DEV, KC * M).swapaxes(0, 1)


def solution(mesh):
    in_specs = (
        P("wide", None, "narrow", None),
        P("wide", "narrow"),
        P("wide", None),
        P("wide", None),
        P("wide", None),
        P("wide"),
    )
    out_specs = P("wide", "narrow", None)
    return jax.shard_map(
        on_device, mesh=mesh, in_specs=in_specs, out_specs=out_specs, check_vma=False
    )
```

```python
import functools

import jax
import jax.numpy as jnp
from jax import lax
from jax.experimental import pallas as pl
from jax.experimental.pallas import tpu as pltpu
from jax.sharding import PartitionSpec as P

B = 192
M = 48
KC = 8
AGG_DEV = 16
LANES = 128
GROUP = 4
SEATS = 8
CUTS = 3
EIGHT = 8
MESH = pl.DeviceIdType.MESH
F32 = jnp.float32
BF16 = jnp.bfloat16
I32 = jnp.int32
NT = (((1,), (1,)), ((), ()))
TWIN, OWN, SKEW = 0, 1, 2
VIA_X = 4


def kernel(
    count, parts,
    col_ref, slot_ref, owner_ref, local_ref, raw_ref, op_hbm, out_ref,
    op_ref, rawf, flat, held, tall, spread, tmp, part, rx1, tx2, rx2, sm, rxs, meta, seats, expand, pk, rxw,
    op_sem, gs, gr, ns, nr, ys, yr, ws, wr, ks,
):
    wide = lax.axis_index("wide")
    me = lax.axis_index("narrow")
    near = me + 1 - 2 * (me % 2)
    far = (me + 2) % parts
    cross = (near + 2) % parts
    odd = wide % 2
    twin = wide + 1 - 2 * odd
    half = count // 2
    rows, terms, depth, _ = op_ref.shape
    side = M // parts
    cut = side // CUTS
    block = cut * AGG_DEV
    chunks = rows // EIGHT
    groups = rows // GROUP
    halves = groups // SEATS
    ahead = wide + 2 - 4 * odd
    has_ahead = (ahead >= 0) & (ahead < count)
    behind = wide - 2 + 4 * odd
    has_behind = (behind >= 0) & (behind < count)

    def remote(src, dst, s, r, target):
        return pltpu.make_async_remote_copy(
            src_ref=src, dst_ref=dst, send_sem=s, recv_sem=r, device_id=target, device_id_type=MESH
        )

    fetch = pltpu.make_async_copy(op_hbm, op_ref, op_sem)
    fetch.start()

    barrier = pltpu.get_barrier_semaphore()

    def hello(where):
        pl.semaphore_signal(barrier, inc=1, device_id=where, device_id_type=MESH)

    hello((wide, near))
    hello((wide, far))
    hello((twin, me))

    @pl.loop(1, half)
    def _(d):
        hello(((wide + 2 * d) % count, me))

    width = depth * M
    rawf[:, :width] = raw_ref[...].astype(F32)
    rawf[:, width:] = jnp.zeros((rows, LANES), F32)
    for b in range(depth):
        flat[pl.ds(b, rows, stride=depth), :] = rawf[:, b * M : b * M + LANES]
    eye = (
        lax.broadcasted_iota(I32, (M, M), 0) == lax.broadcasted_iota(I32, (M, M), 1)
    ).astype(F32).astype(BF16)
    step = EIGHT * depth
    for c in range(chunks):
        blocks = flat[c * step : (c + 1) * step, :M].astype(BF16)
        held[OWN, me, c] = lax.dot_general(eye, blocks, NT, preferred_element_type=F32).astype(BF16)
    meta[0] = jnp.zeros((8, LANES), F32)
    meta[0, :terms, :rows] = slot_ref[...].astype(F32)
    meta[0, terms : terms + 1, :rows] = owner_ref[...].astype(F32)
    meta[0, terms + 1 : terms + 2, :rows] = local_ref[...].astype(F32)

    pl.semaphore_wait(barrier, half + 2)

    def move(slot, kind, c, target, source, share):
        return remote(
            held.at[source, share, c], held.at[slot, share, c],
            gs.at[slot, kind, c], gr.at[slot, kind, c], target,
        )

    def along(slot, c):
        if slot == TWIN:
            return move(TWIN, 0, c, (twin, me), OWN, me)
        return move(SKEW, 0, c, (ahead, me), TWIN, me)

    def along_far(slot, c):
        if slot == TWIN:
            return move(TWIN, 1, c, (twin, me), OWN, far)
        return move(SKEW, 1, c, (ahead, me), TWIN, far)

    def to_far(slot, c):
        return move(slot, 1, c, (wide, far), slot, me)

    def to_near(slot, c):
        return move(slot, 2, c, (wide, near), slot, me)

    def far_to_near(slot, c):
        return move(slot, 3, c, (wide, near), slot, far)

    def by_x(c):
        return c >= chunks - VIA_X

    def keys():
        return remote(meta.at[0], meta.at[1], ks.at[0], ks.at[1], (twin, me))

    for c in range(chunks):
        along(TWIN, c).start()
        to_far(OWN, c).start()
        to_near(OWN, c).start()
    keys().start()

    c_at = lax.broadcasted_iota(I32, (M, 2 * LANES), 0)
    lane = lax.broadcasted_iota(I32, (M, 2 * LANES), 1)
    c_part = c_at // side
    c_in = c_at - c_part * side
    c_cut = c_in // cut
    c_seat = (c_part % 2) * CUTS + c_cut
    c_lane = (c_part // 2) * LANES + c_in - c_cut * cut
    for seat in range(SEATS):
        first_lane = c_lane + ((c_seat + seat) % SEATS) * (GROUP * cut)
        for j in range(GROUP):
            chosen = (lane == first_lane + j * cut).astype(F32).astype(BF16)
            for h in range(halves):
                i = (h * SEATS + seat) * GROUP + j
                spread[h * SEATS + seat, j * depth : (j + 1) * depth] = jnp.dot(
                    flat[i * depth : (i + 1) * depth, :M].astype(BF16), chosen,
                    preferred_element_type=F32,
                ).astype(BF16)

    base_of = {OWN: rows, TWIN: (1 - odd) * (2 * rows), SKEW: odd * (2 * rows)}

    def assemble(slot, c):
        base = base_of[slot] + c * EIGHT
        for i in range(EIGHT):
            tall[base + i] = jnp.concatenate(
                [held[slot, p, c, :, i * depth : (i + 1) * depth] for p in range(parts)], axis=1
            )

    def pair(slot, c):
        to_near(slot, c).wait()
        far_to_near(slot, c).wait()

    for c in range(chunks):
        to_far(OWN, c).wait_recv()
        far_to_near(OWN, c).start()
        if not by_x(c):
            along_far(TWIN, c).start()
        along(TWIN, c).wait_recv()
        pl.when(has_ahead)(lambda: along(SKEW, c).start())
        if by_x(c):
            to_far(TWIN, c).start()
        to_near(TWIN, c).start()
    for c in range(chunks):
        @pl.when(has_behind)
        def _():
            along(SKEW, c).wait_recv()
            if by_x(c):
                to_far(SKEW, c).start()
            to_near(SKEW, c).start()

        (to_far if by_x(c) else along_far)(TWIN, c).wait_recv()
        if not by_x(c):
            pl.when(has_ahead)(lambda: along_far(SKEW, c).start())
        far_to_near(TWIN, c).start()
        pair(OWN, c)
        assemble(OWN, c)
    for c in range(chunks):
        pair(TWIN, c)
        assemble(TWIN, c)

        @pl.when(has_behind)
        def _():
            (to_far if by_x(c) else along_far)(SKEW, c).wait_recv()
            far_to_near(SKEW, c).start()

    @pl.when(has_behind)
    def _():
        for c in range(chunks):
            pair(SKEW, c)
            assemble(SKEW, c)

    fetch.wait()

    def first(q, h):
        return remote(part.at[cross, q, h], rx1.at[1, q, h], ns.at[0, q, h], nr.at[0, q, h], (wide, near))

    def second(q, h):
        return remote(part.at[near, q, h], rx1.at[0, q, h], ns.at[1, q, h], nr.at[1, q, h], (wide, near))

    def third(q, h):
        return remote(tx2.at[q, h], rx2.at[q, h], ns.at[2, q, h], nr.at[2, q, h], (wide, far))

    def fourth(q, h):
        return remote(sm.at[q, h], rxs.at[q, h], ys.at[q, h], yr.at[q, h], (twin, me))

    def relay(q, h):
        first(q, h).wait()
        tx2[q, h] = (part[far, q, h] + rx1[1, q, h]).astype(BF16)
        third(q, h).start()

    def finish(q, h):
        second(q, h).wait()
        third(q, h).wait()
        sm[q, h] = (part[me, q, h] + rx1[0, q, h] + rx2[q, h].astype(F32)).astype(BF16)
        fourth(q, h).start()

    tile = GROUP * depth
    tile_lane = lax.broadcasted_iota(I32, (M, tile), 1)
    shift = rows - wide * rows

    def products(h, seat):
        start = (h * SEATS + seat) * GROUP
        applied = []
        for k in range(terms):
            left = jnp.concatenate(
                [tall[jnp.maximum(col_ref[k, start + j] + shift, 0)] for j in range(GROUP)], axis=0
            )
            right = jnp.concatenate([op_ref[start + j, k] for j in range(GROUP)], axis=0)
            both = lax.dot_general(left, right, NT, preferred_element_type=F32)
            kept = both[(GROUP - 1) * M :]
            for j in range(GROUP - 2, -1, -1):
                kept = jnp.where(tile_lane < (j + 1) * depth, both[j * M : (j + 1) * M], kept)
            applied.append(kept.astype(BF16))
        tmp[seat] = jnp.dot(
            jnp.concatenate(applied, axis=0), spread[h * SEATS + seat], preferred_element_type=F32
        )

    seat_lane = lax.broadcasted_iota(I32, (M, LANES), 1) // (GROUP * cut)

    def deal(h):
        @pl.loop(0, terms)
        def _(k):
            r = pl.ds(pl.multiple_of(k * M, M), M)
            for pair_at in range(parts // 2):
                held_at = [tmp[s, r, pair_at * LANES : (pair_at + 1) * LANES] for s in range(SEATS)]
                bit = 1
                while bit < SEATS:
                    taken = (seat_lane // bit) % 2 == 1
                    held_at = [
                        jnp.where(taken, held_at[(s + bit) % SEATS], held_at[s]) for s in range(SEATS)
                    ]
                    bit *= 2
                for s in range(2 * CUTS):
                    part[pair_at * 2 + s // CUTS, s % CUTS, h, r] = held_at[-s % SEATS]

    for h in range(halves):
        for seat in range(SEATS):
            products(h, seat)
            if h > 0 and seat == SEATS // 2:
                relay(0, h - 1)
        deal(h)
        for q in range(CUTS):
            first(q, h).start()
            second(q, h).start()

    order = [(q, h) for q in range(CUTS) for h in range(halves)]
    for q, h in order[1:]:
        relay(q, h)

    keys().wait()
    at = lax.broadcasted_iota(I32, (1, LANES), 1)
    row_at = lax.broadcasted_iota(I32, (LANES, LANES), 0)
    for q in range(CUTS):
        for h in range(halves):
            seat = (at // (GROUP * cut) - ((me % 2) * CUTS + q) + SEATS) % SEATS
            row = (h * SEATS + seat) * GROUP + (at // cut) % GROUP
            picks = (row_at == row).astype(F32).astype(BF16)
            for who in range(2):
                seen = jnp.dot(meta[who].astype(BF16), picks, preferred_element_type=F32)
                key = (
                    seen[terms : terms + 1] * block
                    + (at % cut).astype(F32) * AGG_DEV
                    + seen[terms + 1 : terms + 2]
                )
                seats[who, q, h] = jnp.concatenate([seen[:terms], key, key], axis=0)

    def widen(who, source, q):
        @pl.loop(0, halves)
        def _(h):
            blocks = [source[q, h, k * M : (k + 1) * M].astype(F32) for k in range(terms)]
            slots = [seats[who, q, h, k : k + 1] for k in range(terms)]
            for s in range(KC):
                total = jnp.zeros((M, LANES), F32)
                for k in range(terms):
                    total = total + jnp.where(slots[k] == s, blocks[k], 0.0)
                expand[who, h, s * M : (s + 1) * M] = total.astype(BF16)

    place = lax.broadcasted_iota(I32, (block, LANES), 0)

    def dense(owner, q):
        total = jnp.zeros((block, KC * M), F32)
        for who in range(2):
            for h in range(halves):
                hot = seats[who, q, h, terms : terms + 1] == (place + owner * block).astype(F32)
                total = total + lax.dot_general(
                    hot.astype(F32).astype(BF16), expand[who, h], NT, preferred_element_type=F32
                )
        return total

    def send(q, d):
        return remote(pk.at[q, d], rxw.at[q, d], ws.at[q, d], wr.at[q, d], ((wide + 2 * d) % count, me))

    def turn(i):
        return 1 + (i + half // 2 - 1) % (half - 1)

    for h in range(halves):
        finish(0, h)
    for q in range(CUTS):
        if q + 1 < CUTS:
            for h in range(halves):
                finish(q + 1, h)
        widen(0, sm, q)
        for h in range(halves):
            fourth(q, h).wait()
        widen(1, rxs, q)

        @pl.loop(0, half - 1)
        def _(i):
            d = turn(i)
            pk[q, d] = dense((wide + 2 * d) % count, q).astype(BF16)
            send(q, d).start()

        out_ref[q * block : (q + 1) * block] = dense(wide, q)

    for q in range(CUTS):
        @pl.loop(0, half - 1)
        def _(i):
            d = turn(i)
            send(q, d).wait()
            out_ref[q * block : (q + 1) * block] += rxw[q, d].astype(F32)

    for c in range(chunks):
        along(TWIN, c).wait_send()
        to_far(OWN, c).wait_send()
        if by_x(c):
            to_far(TWIN, c).wait_send()
        else:
            along_far(TWIN, c).wait_send()

        @pl.when(has_ahead)
        def _():
            along(SKEW, c).wait_send()
            if not by_x(c):
                along_far(SKEW, c).wait_send()

        if by_x(c):
            pl.when(has_behind)(lambda: to_far(SKEW, c).wait_send())


def on_device(op_blocks, prolong, col_index, slot_index, dest_owner, dest_local):
    rows, terms, depth, _ = op_blocks.shape
    count = lax.axis_size("wide")
    parts = lax.axis_size("narrow")
    side = M // parts
    chunks = rows // EIGHT
    groups = rows // GROUP
    halves = groups // SEATS
    half = count // 2
    block = side // CUTS * AGG_DEV
    deep = terms * M
    vmem = pl.BlockSpec(memory_space=pltpu.VMEM)
    smem = pl.BlockSpec(memory_space=pltpu.SMEM)
    hbm = pl.BlockSpec(memory_space=pl.ANY)
    dma = pltpu.SemaphoreType.DMA
    unit = (CUTS, halves, deep, LANES)
    coarse = pl.pallas_call(
        functools.partial(kernel, count, parts),
        out_shape=jax.ShapeDtypeStruct((side * AGG_DEV, KC * M), F32),
        in_specs=[smem, vmem, vmem, vmem, vmem, hbm],
        out_specs=vmem,
        scratch_shapes=[
            pltpu.VMEM(op_blocks.shape, BF16),
            pltpu.VMEM((rows, depth * M + LANES), F32),
            pltpu.VMEM((rows * depth, LANES), F32),
            pltpu.VMEM((3, parts, chunks, M, EIGHT * depth), BF16),
            pltpu.VMEM((3 * rows, M, B), BF16),
            pltpu.VMEM((groups, GROUP * depth, 2 * LANES), BF16),
            pltpu.VMEM((SEATS, deep, 2 * LANES), F32),
            pltpu.VMEM((parts,) + unit, F32),
            pltpu.VMEM((2,) + unit, F32),
            pltpu.VMEM(unit, BF16),
            pltpu.VMEM(unit, BF16),
            pltpu.VMEM(unit, BF16),
            pltpu.VMEM(unit, BF16),
            pltpu.VMEM((2, 8, LANES), F32),
            pltpu.VMEM((2, CUTS, halves, 8, LANES), F32),
            pltpu.VMEM((2, halves, KC * M, LANES), BF16),
            pltpu.VMEM((CUTS, half, block, KC * M), BF16),
            pltpu.VMEM((CUTS, half, block, KC * M), BF16),
            dma,
            dma((3, 4, chunks)), dma((3, 4, chunks)),
            dma((3, CUTS, halves)), dma((3, CUTS, halves)),
            dma((CUTS, halves)), dma((CUTS, halves)),
            dma((CUTS, half)), dma((CUTS, half)), dma((2,)),
        ],
        compiler_params=pltpu.CompilerParams(
            collective_id=0, has_side_effects=True, vmem_limit_bytes=52 << 20
        ),
    )(
        col_index.T, slot_index.T, dest_owner.T, dest_local.reshape(1, -1), prolong, op_blocks
    )
    return coarse.reshape(side, AGG_DEV, KC * M).swapaxes(0, 1)


def solution(mesh):
    in_specs = (
        P("wide", None, "narrow", None),
        P("wide", "narrow"),
        P("wide", None),
        P("wide", None),
        P("wide", None),
        P("wide"),
    )
    out_specs = P("wide", "narrow", None)
    return jax.shard_map(
        on_device, mesh=mesh, in_specs=in_specs, out_specs=out_specs, check_vma=False
    )
```

```python
import functools

import jax
import jax.numpy as jnp
from jax import lax
from jax.experimental import pallas as pl
from jax.experimental.pallas import tpu as pltpu
from jax.sharding import PartitionSpec as P

B = 192
M = 48
KC = 8
AGG_DEV = 16
LANES = 128
GROUP = 4
SEATS = 8
CUTS = 3
EIGHT = 8
MESH = pl.DeviceIdType.MESH
F32 = jnp.float32
BF16 = jnp.bfloat16
I32 = jnp.int32
NT = (((1,), (1,)), ((), ()))
TWIN, OWN, SKEW = 0, 1, 2
VIA_X = 4


def kernel(
    count, parts,
    col_ref, slot_ref, owner_ref, local_ref, raw_ref, op_hbm, out_ref,
    op_ref, rawf, flat, held, tall, spread, tmp, part, rx1, tx2, rx2, sm, rxs, meta, seats, expand, pk, rxw,
    op_sem, gs, gr, ns, nr, ys, yr, ws, wr, ks,
):
    wide = lax.axis_index("wide")
    me = lax.axis_index("narrow")
    near = me + 1 - 2 * (me % 2)
    far = (me + 2) % parts
    cross = (near + 2) % parts
    odd = wide % 2
    twin = wide + 1 - 2 * odd
    half = count // 2
    rows, terms, depth, _ = op_ref.shape
    side = M // parts
    cut = side // CUTS
    block = cut * AGG_DEV
    chunks = rows // EIGHT
    groups = rows // GROUP
    halves = groups // SEATS
    ahead = wide + 2 - 4 * odd
    has_ahead = (ahead >= 0) & (ahead < count)
    behind = wide - 2 + 4 * odd
    has_behind = (behind >= 0) & (behind < count)

    def remote(src, dst, s, r, target):
        return pltpu.make_async_remote_copy(
            src_ref=src, dst_ref=dst, send_sem=s, recv_sem=r, device_id=target, device_id_type=MESH
        )

    fetch = pltpu.make_async_copy(op_hbm, op_ref, op_sem)
    fetch.start()

    barrier = pltpu.get_barrier_semaphore()

    def hello(where):
        pl.semaphore_signal(barrier, inc=1, device_id=where, device_id_type=MESH)

    hello((wide, near))
    hello((wide, far))
    hello((twin, me))

    @pl.loop(1, half)
    def _(d):
        hello(((wide + 2 * d) % count, me))

    width = depth * M
    rawf[:, :width] = raw_ref[...].astype(F32)
    rawf[:, width:] = jnp.zeros((rows, LANES), F32)
    for b in range(depth):
        flat[pl.ds(b, rows, stride=depth), :] = rawf[:, b * M : b * M + LANES]
    eye = (
        lax.broadcasted_iota(I32, (M, M), 0) == lax.broadcasted_iota(I32, (M, M), 1)
    ).astype(F32).astype(BF16)
    step = EIGHT * depth
    for c in range(chunks):
        blocks = flat[c * step : (c + 1) * step, :M].astype(BF16)
        held[OWN, me, c] = lax.dot_general(eye, blocks, NT, preferred_element_type=F32).astype(BF16)
    meta[0] = jnp.zeros((8, LANES), F32)
    meta[0, :terms, :rows] = slot_ref[...].astype(F32)
    meta[0, terms : terms + 1, :rows] = owner_ref[...].astype(F32)
    meta[0, terms + 1 : terms + 2, :rows] = local_ref[...].astype(F32)

    pl.semaphore_wait(barrier, half + 2)

    def move(slot, kind, c, target, source, share):
        return remote(
            held.at[source, share, c], held.at[slot, share, c],
            gs.at[slot, kind, c], gr.at[slot, kind, c], target,
        )

    def along(slot, c):
        if slot == TWIN:
            return move(TWIN, 0, c, (twin, me), OWN, me)
        return move(SKEW, 0, c, (ahead, me), TWIN, me)

    def along_far(slot, c):
        if slot == TWIN:
            return move(TWIN, 1, c, (twin, me), OWN, far)
        return move(SKEW, 1, c, (ahead, me), TWIN, far)

    def to_far(slot, c):
        return move(slot, 1, c, (wide, far), slot, me)

    def to_near(slot, c):
        return move(slot, 2, c, (wide, near), slot, me)

    def far_to_near(slot, c):
        return move(slot, 3, c, (wide, near), slot, far)

    def by_x(c):
        return c >= chunks - VIA_X

    def keys():
        return remote(meta.at[0], meta.at[1], ks.at[0], ks.at[1], (twin, me))

    for c in range(chunks):
        along(TWIN, c).start()
        to_far(OWN, c).start()
        to_near(OWN, c).start()
    keys().start()

    c_at = lax.broadcasted_iota(I32, (M, 2 * LANES), 0)
    lane = lax.broadcasted_iota(I32, (M, 2 * LANES), 1)
    c_part = c_at // side
    c_in = c_at - c_part * side
    c_cut = c_in // cut
    c_seat = (c_part % 2) * CUTS + c_cut
    c_lane = (c_part // 2) * LANES + c_in - c_cut * cut
    for seat in range(SEATS):
        first_lane = c_lane + ((c_seat + seat) % SEATS) * (GROUP * cut)
        for j in range(GROUP):
            chosen = (lane == first_lane + j * cut).astype(F32).astype(BF16)
            for h in range(halves):
                i = (h * SEATS + seat) * GROUP + j
                spread[h * SEATS + seat, j * depth : (j + 1) * depth] = jnp.dot(
                    flat[i * depth : (i + 1) * depth, :M].astype(BF16), chosen,
                    preferred_element_type=F32,
                ).astype(BF16)

    base_of = {OWN: rows, TWIN: (1 - odd) * (2 * rows), SKEW: odd * (2 * rows)}

    def assemble(slot, c):
        base = base_of[slot] + c * EIGHT
        for i in range(EIGHT):
            tall[base + i] = jnp.concatenate(
                [held[slot, p, c, :, i * depth : (i + 1) * depth] for p in range(parts)], axis=1
            )

    def pair(slot, c):
        to_near(slot, c).wait()
        far_to_near(slot, c).wait()

    for c in range(chunks):
        to_far(OWN, c).wait_recv()
        far_to_near(OWN, c).start()
        if not by_x(c):
            along_far(TWIN, c).start()
        along(TWIN, c).wait_recv()
        pl.when(has_ahead)(lambda: along(SKEW, c).start())
        if by_x(c):
            to_far(TWIN, c).start()
        to_near(TWIN, c).start()
    for c in range(chunks):
        @pl.when(has_behind)
        def _():
            along(SKEW, c).wait_recv()
            if by_x(c):
                to_far(SKEW, c).start()
            to_near(SKEW, c).start()

        (to_far if by_x(c) else along_far)(TWIN, c).wait_recv()
        if not by_x(c):
            pl.when(has_ahead)(lambda: along_far(SKEW, c).start())
        far_to_near(TWIN, c).start()
        pair(OWN, c)
        assemble(OWN, c)
    for c in range(chunks):
        pair(TWIN, c)
        assemble(TWIN, c)

        @pl.when(has_behind)
        def _():
            (to_far if by_x(c) else along_far)(SKEW, c).wait_recv()
            far_to_near(SKEW, c).start()

    @pl.when(has_behind)
    def _():
        for c in range(chunks):
            pair(SKEW, c)
            assemble(SKEW, c)

    fetch.wait()

    def first(q, h):
        return remote(part.at[cross, q, h], rx1.at[1, q, h], ns.at[0, q, h], nr.at[0, q, h], (wide, near))

    def second(q, h):
        return remote(part.at[near, q, h], rx1.at[0, q, h], ns.at[1, q, h], nr.at[1, q, h], (wide, near))

    def third(q, h):
        return remote(tx2.at[q, h], rx2.at[q, h], ns.at[2, q, h], nr.at[2, q, h], (wide, far))

    def fourth(q, h):
        return remote(sm.at[q, h], rxs.at[q, h], ys.at[q, h], yr.at[q, h], (twin, me))

    def relay(q, h):
        first(q, h).wait()
        tx2[q, h] = (part[far, q, h] + rx1[1, q, h]).astype(BF16)
        third(q, h).start()

    def finish(q, h):
        second(q, h).wait()
        third(q, h).wait()
        sm[q, h] = (part[me, q, h] + rx1[0, q, h] + rx2[q, h].astype(F32)).astype(BF16)
        fourth(q, h).start()

    tile = GROUP * depth
    tile_lane = lax.broadcasted_iota(I32, (M, tile), 1)
    shift = rows - wide * rows

    def products(h, seat):
        start = (h * SEATS + seat) * GROUP
        applied = []
        for k in range(terms):
            left = jnp.concatenate(
                [tall[jnp.maximum(col_ref[k, start + j] + shift, 0)] for j in range(GROUP)], axis=0
            )
            right = jnp.concatenate([op_ref[start + j, k] for j in range(GROUP)], axis=0)
            both = lax.dot_general(left, right, NT, preferred_element_type=F32)
            kept = both[(GROUP - 1) * M :]
            for j in range(GROUP - 2, -1, -1):
                kept = jnp.where(tile_lane < (j + 1) * depth, both[j * M : (j + 1) * M], kept)
            applied.append(kept.astype(BF16))
        tmp[seat] = jnp.dot(
            jnp.concatenate(applied, axis=0), spread[h * SEATS + seat], preferred_element_type=F32
        )

    seat_lane = lax.broadcasted_iota(I32, (M, LANES), 1) // (GROUP * cut)

    def deal(h):
        @pl.loop(0, terms)
        def _(k):
            r = pl.ds(pl.multiple_of(k * M, M), M)
            for pair_at in range(parts // 2):
                held_at = [tmp[s, r, pair_at * LANES : (pair_at + 1) * LANES] for s in range(SEATS)]
                bit = 1
                while bit < SEATS:
                    taken = (seat_lane // bit) % 2 == 1
                    held_at = [
                        jnp.where(taken, held_at[(s + bit) % SEATS], held_at[s]) for s in range(SEATS)
                    ]
                    bit *= 2
                for s in range(2 * CUTS):
                    part[pair_at * 2 + s // CUTS, s % CUTS, h, r] = held_at[-s % SEATS]

    for h in range(halves):
        for seat in range(SEATS):
            products(h, seat)
            if h > 0 and seat == SEATS // 2:
                relay(0, h - 1)
            if h > 0 and seat == SEATS - 2:
                relay(1, h - 1)
        deal(h)
        for q in range(CUTS):
            first(q, h).start()
        for q in range(CUTS):
            second(q, h).start()

    order = [(q, h) for q in range(CUTS) for h in range(halves)]
    for q, h in order[1:]:
        if (q, h) != (1, 0):
            relay(q, h)

    keys().wait()
    at = lax.broadcasted_iota(I32, (1, LANES), 1)
    row_at = lax.broadcasted_iota(I32, (LANES, LANES), 0)
    for q in range(CUTS):
        for h in range(halves):
            seat = (at // (GROUP * cut) - ((me % 2) * CUTS + q) + SEATS) % SEATS
            row = (h * SEATS + seat) * GROUP + (at // cut) % GROUP
            picks = (row_at == row).astype(F32).astype(BF16)
            for who in range(2):
                seen = jnp.dot(meta[who].astype(BF16), picks, preferred_element_type=F32)
                key = (
                    seen[terms : terms + 1] * block
                    + (at % cut).astype(F32) * AGG_DEV
                    + seen[terms + 1 : terms + 2]
                )
                seats[who, q, h] = jnp.concatenate([seen[:terms], key, key], axis=0)

    def widen(who, source, q):
        @pl.loop(0, halves)
        def _(h):
            blocks = [source[q, h, k * M : (k + 1) * M].astype(F32) for k in range(terms)]
            slots = [seats[who, q, h, k : k + 1] for k in range(terms)]
            for s in range(KC):
                total = jnp.zeros((M, LANES), F32)
                for k in range(terms):
                    total = total + jnp.where(slots[k] == s, blocks[k], 0.0)
                expand[who, h, s * M : (s + 1) * M] = total.astype(BF16)

    place = lax.broadcasted_iota(I32, (block, LANES), 0)

    def dense(owner, q):
        total = jnp.zeros((block, KC * M), F32)
        for who in range(2):
            for h in range(halves):
                hot = seats[who, q, h, terms : terms + 1] == (place + owner * block).astype(F32)
                total = total + lax.dot_general(
                    hot.astype(F32).astype(BF16), expand[who, h], NT, preferred_element_type=F32
                )
        return total

    def send(q, d):
        return remote(pk.at[q, d], rxw.at[q, d], ws.at[q, d], wr.at[q, d], ((wide + 2 * d) % count, me))

    def turn(i):
        return 1 + (i + half // 2 - 1) % (half - 1)

    for h in range(halves):
        finish(0, h)
    for q in range(CUTS):
        if q + 1 < CUTS:
            for h in range(halves):
                finish(q + 1, h)
        widen(0, sm, q)
        for h in range(halves):
            fourth(q, h).wait()
        widen(1, rxs, q)

        @pl.loop(0, half - 1)
        def _(i):
            d = turn(i)
            pk[q, d] = dense((wide + 2 * d) % count, q).astype(BF16)
            send(q, d).start()

        out_ref[q * block : (q + 1) * block] = dense(wide, q)

    for q in range(CUTS):
        @pl.loop(0, half - 1)
        def _(i):
            d = turn(i)
            send(q, d).wait()
            out_ref[q * block : (q + 1) * block] += rxw[q, d].astype(F32)

    for c in range(chunks):
        along(TWIN, c).wait_send()
        to_far(OWN, c).wait_send()
        if by_x(c):
            to_far(TWIN, c).wait_send()
        else:
            along_far(TWIN, c).wait_send()

        @pl.when(has_ahead)
        def _():
            along(SKEW, c).wait_send()
            if not by_x(c):
                along_far(SKEW, c).wait_send()

        if by_x(c):
            pl.when(has_behind)(lambda: to_far(SKEW, c).wait_send())


def on_device(op_blocks, prolong, col_index, slot_index, dest_owner, dest_local):
    rows, terms, depth, _ = op_blocks.shape
    count = lax.axis_size("wide")
    parts = lax.axis_size("narrow")
    side = M // parts
    chunks = rows // EIGHT
    groups = rows // GROUP
    halves = groups // SEATS
    half = count // 2
    block = side // CUTS * AGG_DEV
    deep = terms * M
    vmem = pl.BlockSpec(memory_space=pltpu.VMEM)
    smem = pl.BlockSpec(memory_space=pltpu.SMEM)
    hbm = pl.BlockSpec(memory_space=pl.ANY)
    dma = pltpu.SemaphoreType.DMA
    unit = (CUTS, halves, deep, LANES)
    coarse = pl.pallas_call(
        functools.partial(kernel, count, parts),
        out_shape=jax.ShapeDtypeStruct((side * AGG_DEV, KC * M), F32),
        in_specs=[smem, vmem, vmem, vmem, vmem, hbm],
        out_specs=vmem,
        scratch_shapes=[
            pltpu.VMEM(op_blocks.shape, BF16),
            pltpu.VMEM((rows, depth * M + LANES), F32),
            pltpu.VMEM((rows * depth, LANES), F32),
            pltpu.VMEM((3, parts, chunks, M, EIGHT * depth), BF16),
            pltpu.VMEM((3 * rows, M, B), BF16),
            pltpu.VMEM((groups, GROUP * depth, 2 * LANES), BF16),
            pltpu.VMEM((SEATS, deep, 2 * LANES), F32),
            pltpu.VMEM((parts,) + unit, F32),
            pltpu.VMEM((2,) + unit, F32),
            pltpu.VMEM(unit, BF16),
            pltpu.VMEM(unit, BF16),
            pltpu.VMEM(unit, BF16),
            pltpu.VMEM(unit, BF16),
            pltpu.VMEM((2, 8, LANES), F32),
            pltpu.VMEM((2, CUTS, halves, 8, LANES), F32),
            pltpu.VMEM((2, halves, KC * M, LANES), BF16),
            pltpu.VMEM((CUTS, half, block, KC * M), BF16),
            pltpu.VMEM((CUTS, half, block, KC * M), BF16),
            dma,
            dma((3, 4, chunks)), dma((3, 4, chunks)),
            dma((3, CUTS, halves)), dma((3, CUTS, halves)),
            dma((CUTS, halves)), dma((CUTS, halves)),
            dma((CUTS, half)), dma((CUTS, half)), dma((2,)),
        ],
        compiler_params=pltpu.CompilerParams(
            collective_id=0, has_side_effects=True, vmem_limit_bytes=52 << 20
        ),
    )(
        col_index.T, slot_index.T, dest_owner.T, dest_local.reshape(1, -1), prolong, op_blocks
    )
    return coarse.reshape(side, AGG_DEV, KC * M).swapaxes(0, 1)


def solution(mesh):
    in_specs = (
        P("wide", None, "narrow", None),
        P("wide", "narrow"),
        P("wide", None),
        P("wide", None),
        P("wide", None),
        P("wide"),
    )
    out_specs = P("wide", "narrow", None)
    return jax.shard_map(
        on_device, mesh=mesh, in_specs=in_specs, out_specs=out_specs, check_vma=False
    )
```
